768 devices in a mesh: tiles: 192 (over y, z, core), band: 4 (over x).
Axes of the slice: x: 4, y: 8, z: 12, core: 2. Of those that a mesh axis runs over, the one named last changes fastest.
Arguments:
- optical_depth: bfloat16 [3072, 90, 4, 512], P('tiles', None, None, 'band'), may hold values from 0.00049972534 to 0.029907227
- albedo: bfloat16 [3072, 90, 512], P('tiles', None, 'band'), may hold values from 0.69921875 to 0.96875
- insolation: bfloat16 [3072, 512], P('tiles', 'band'), may hold values from 20 to 100
- sunlit: int32 [3072, 4], P('tiles', 'band'), may hold values from 0 to 1, as said below
- point_weight: float32 [4], replicated, may hold values from 0.1 to 1
- anomaly: float32 [3072, 90, 512], P('tiles', None, 'band'), may hold values from -6 to 6
Outputs:
- heating: float32 [3072, 90, 512], P('tiles', None, 'band')
- smoothed: float32 [3072, 90, 512], P('tiles', None, 'band')
The draws below stay inside these ranges and needn't reach their ends.
Inputs may be any that keep to these rules, and one draw needn't show every extreme that they name: In every row, of two blocks that lie half of 4 sectors apart, exactly one is sunlit.
All inputs are finite; a program needn't handle non-finite values.
Results may differ from the reference program's by a relative error of at most 0.00045.
Values may be sent and summed in bfloat16 or wider, within the bound.
No kernel may reach another device: no remote copies, remote signals or barrier semaphores. Data moves between devices by JAX's collectives and lax.ppermute only.
A program may use at most 64 MiB of HBM per device.

```python
import math
import jax
import jax.numpy as jnp
from jax import lax

ROWS_DEV = 16
BLOCK = 128
LEV = 90
G = 4
DIFF_STEPS = 4
NROWS = 3072
SECTORS = 4
NCOLS = 512


def draw_sunlit(key, part):
    key_start = jax.random.fold_in(key, 11)
    key_flip = jax.random.fold_in(key, 23)
    day_start = jax.random.randint(key_start, (), 0, SECTORS)
    half_sectors = SECTORS // 2
    sector_ids = jnp.arange(half_sectors, dtype=jnp.int32)
    is_day = (sector_ids - day_start) % SECTORS < half_sectors
    flipped = jax.random.randint(key_flip, (NROWS, half_sectors), 0, 8) == 0
    day_first = jnp.logical_xor(is_day[None, :], flipped)
    daylit = jnp.concatenate([day_first, jnp.logical_not(day_first)], axis=1)
    return daylit.astype(jnp.int32)


def level_of(stream_key, dims, cuts, low, top_value):
    gain, own = 1.0, jax.random.fold_in(stream_key, 6)
    for dim, parts in cuts:
        draws = jnp.exp(jax.random.uniform(jax.random.fold_in(own, dim), (parts,), jnp.float32, low / len(cuts), top_value / len(cuts)))
        gain = gain * jnp.repeat(draws, dims[dim] // parts).reshape([-1 if axis == dim else 1 for axis in range(len(dims))])
    return gain


def gaussian(own_key, shape, scale, bound, split=(), kind=jnp.bfloat16):
    level = level_of(own_key, shape, split, -0.22, 0.18) if split else 1.0
    result = jax.random.normal(own_key, shape, jnp.float32) * scale * level
    return jnp.minimum(jnp.maximum(result, -bound), bound).astype(kind)


def setup_inputs(seed: int = 0) -> dict:
    key_list = jax.random.split(jax.random.key(seed), 7)
    optical_depth = jnp.clip(jnp.exp(math.log(0.029907227) - 4.091797 * jax.random.uniform(key_list[0], (NROWS, LEV, G, NCOLS), jnp.float32) ** level_of(key_list[0], (NROWS, LEV, G, NCOLS), ((0, 192), (3, 4)), -0.2, 0.2)), 0.00049972534, 0.029907227).astype(jnp.bfloat16)
    albedo = jnp.clip(0.69921875 + 0.26953125 * jax.random.uniform(key_list[1], (NROWS, LEV, NCOLS), jnp.float32) ** level_of(key_list[1], (NROWS, LEV, NCOLS), ((0, 192), (2, 4)), -0.2, 0.2), 0.69921875, 0.96875).astype(jnp.bfloat16)
    insolation = jnp.clip(20.0 + 80.0 * jax.random.uniform(key_list[2], (NROWS, NCOLS), jnp.float32) ** level_of(key_list[2], (NROWS, NCOLS), ((0, 192), (1, 4)), -0.2, 0.2), 20.0, 100.0).astype(jnp.bfloat16)
    sunlit = draw_sunlit(jax.random.fold_in(key_list[6], 71), 0)
    point_weight = jnp.clip(jnp.exp(jax.random.uniform(key_list[4], (G,), jnp.float32, math.log(0.1), math.log(1.0))), 0.1, 1.0)
    anomaly = gaussian(key_list[5], (NROWS, LEV, NCOLS), 1.0, 6.0, ((0, 192), (2, 4)), jnp.float32)
    return {"optical_depth": optical_depth, "albedo": albedo, "insolation": insolation, "sunlit": sunlit, "point_weight": point_weight, "anomaly": anomaly}


slant_cosine = 0.5
mixing_rate = 0.2
base_loss = 0.005


def radiate(optical_depth, albedo, sunshine, point_weight):
    depth_levels = jnp.moveaxis(optical_depth.astype(jnp.float32), 1, 0)
    albedo_levels = jnp.moveaxis(albedo.astype(jnp.float32), 1, 0)
    albedo_below = jnp.concatenate([albedo_levels[1:], jnp.zeros_like(albedo_levels[:1])], axis=0)
    sun_float = sunshine.astype(jnp.float32)[:, None, :]
    zeros_full = jnp.zeros(depth_levels.shape[1:], jnp.float32)
    zeros_link = jnp.zeros((depth_levels.shape[1], 1, depth_levels.shape[3]), jnp.float32)

    def downward(state_now, layer_in):
        depth_now, link_prev, ratio_prev, swept_prev = state_now
        depth_layer, albedo_now, albedo_next = layer_in
        depth_new = depth_now + depth_layer
        extinct = sun_float * (jnp.exp(-depth_now / slant_cosine) - jnp.exp(-depth_new / slant_cosine))
        link_next = (albedo_now * albedo_next)[:, None, :]
        diagonal = base_loss + 2.0 * (1.0 - albedo_now)[:, None, :] * depth_layer + link_prev + link_next
        pivot = diagonal - link_prev * ratio_prev
        ratio_now = link_next / pivot
        swept_now = (albedo_now[:, None, :] * extinct + link_prev * swept_prev) / pivot
        return (depth_new, link_next, ratio_now, swept_now), (ratio_now, swept_now, extinct)

    init_state = (zeros_full, zeros_link, zeros_full, zeros_full)
    _, (ratios, swept, extinct) = lax.scan(downward, init_state, (depth_levels, albedo_levels, albedo_below))

    def upward(flux_next, layer_in):
        ratio_now, swept_now = layer_in
        diffuse_flux = swept_now + ratio_now * flux_next
        return diffuse_flux, diffuse_flux

    _, diffuse_flux = lax.scan(upward, zeros_full, (ratios, swept), reverse=True)
    absorbed = (1.0 - albedo_levels)[:, :, None, :] * (extinct + 2.0 * depth_levels * diffuse_flux)
    heating = jnp.sum(absorbed * point_weight[None, None, :, None], axis=2)
    return jnp.moveaxis(heating, 0, 1)


def reference(optical_depth, albedo, insolation, sunlit, point_weight, anomaly):
    daylit = jnp.repeat(sunlit, BLOCK, axis=1)
    sunshine = jnp.where(daylit == 1, insolation, jnp.zeros_like(insolation))
    groups = NROWS // ROWS_DEV

    def per_group(inputs):
        return radiate(inputs[0], inputs[1], inputs[2], point_weight)

    heating = lax.map(per_group, (optical_depth.reshape(groups, ROWS_DEV, LEV, G, NCOLS), albedo.reshape(groups, ROWS_DEV, LEV, NCOLS), sunshine.reshape(groups, ROWS_DEV, NCOLS)))
    heating = heating.reshape(NROWS, LEV, NCOLS)
    field_now = anomaly + heating
    for sweep in range(DIFF_STEPS):
        padded = jnp.pad(field_now, ((1, 1), (0, 0), (0, 0)))
        north_south = padded[2:] + padded[:-2]
        east_west = jnp.roll(field_now, 1, axis=2) + jnp.roll(field_now, -1, axis=2)
        field_now = field_now + mixing_rate * (north_south + east_west - 4.0 * field_now)
    return heating, field_now
```

```python
import jax
import jax.numpy as jnp
from jax import lax
from jax.experimental import pallas as pl
from jax.experimental.pallas import tpu as pltpu
from jax.sharding import PartitionSpec as P

DIFF_STEPS = 4
HALO = 4
EDGE = 16
SUB = 8
F32 = jnp.float32
BF16 = jnp.bfloat16
base_loss = 0.005
step_scale = 0.2**DIFF_STEPS


def vmem():
    return pl.BlockSpec(memory_space=pltpu.VMEM)


def smem():
    return pl.BlockSpec(memory_space=pltpu.SMEM)


def radiate_kernel(
    weight_ref, lit_ref, depth_ref, albedo_ref, sun_ref, anomaly_ref,
    heat_ref, field_ref, top_ref, bottom_ref,
    spread_ref, ratio_ref, swept_ref, extinct_ref,
):
    rows, levels, points, width = depth_ref.shape
    per_level = rows * points
    halves = rows // SUB
    chains = halves * points
    sun = sun_ref[...].astype(F32)
    row_ids = lax.broadcasted_iota(jnp.int32, (rows, width), 0)
    lit = jnp.zeros((rows, width), jnp.int32)
    for row in range(rows):
        lit = jnp.where(row_ids == row, lit_ref[row], lit)
    sun = jnp.where(lit == 1, sun, 0.0)
    suns = [sun[h * SUB:(h + 1) * SUB] for h in range(halves)]

    def spread(level):
        for row in range(rows):
            spread_ref[pl.ds(level * per_level + points * row, points), :] = (
                depth_ref[row, level].astype(F32)
            )

    def depth_of(level, half, point):
        start = level * per_level + half * SUB * points + point
        return spread_ref[pl.ds(start, SUB, stride=points), :]

    def albedo_of(level):
        both = albedo_ref[level].astype(F32)
        return [both[h * SUB:(h + 1) * SUB] for h in range(halves)]

    def place(level, chain):
        return pl.ds(pl.multiple_of(level * per_level + chain * SUB, SUB), SUB)

    zero = jnp.zeros((SUB, width), F32)
    one = jnp.ones((SUB, width), F32)

    def down(level, carry):
        link_prev, albedo_now, depth, light, ratio, swept = carry
        last = level == levels - 1
        following = jnp.where(last, level, level + 1)
        spread(following)
        albedo_next = albedo_of(following)
        out = ([], [], [], [], [])
        for half in range(halves):
            albedo = albedo_now[half]
            before = link_prev[half]
            link = jnp.where(last, 0.0, albedo * albedo_next[half])
            slope = 2.0 * (1.0 - albedo)
            level_part = base_loss + before + link
            for point in range(points):
                chain = half * points + point
                layer = depth_of(level, half, point)
                depth_new = depth[chain] + layer
                light_new = jnp.exp(depth_new * -2.0)
                extinct = suns[half] * (light[chain] - light_new)
                inverse = 1.0 / (level_part + slope * layer - before * ratio[chain])
                ratio_new = link * inverse
                swept_new = (albedo * extinct + before * swept[chain]) * inverse
                where = place(level, chain)
                ratio_ref[where, :] = ratio_new
                swept_ref[where, :] = swept_new
                extinct_ref[where, :] = extinct
                for item, value in zip(out, (depth_new, light_new, ratio_new, swept_new)):
                    item.append(value)
            out[4].append(link)
        return (
            tuple(out[4]), tuple(albedo_next), tuple(out[0]), tuple(out[1]), tuple(out[2]),
            tuple(out[3]),
        )

    spread(0)
    lax.fori_loop(
        0, levels, down,
        ((zero,) * halves, tuple(albedo_of(0)), (zero,) * chains, (one,) * chains,
         (zero,) * chains, (zero,) * chains),
    )
    weights = [weight_ref[point] for point in range(points)]

    def up(i, flux):
        level = levels - 1 - i
        albedos = albedo_of(level)
        flux_new = []
        fields = []
        for half in range(halves):
            total = None
            for point in range(points):
                chain = half * points + point
                where = place(level, chain)
                diffuse = swept_ref[where, :] + ratio_ref[where, :] * flux[chain]
                flux_new.append(diffuse)
                layer = depth_of(level, half, point)
                term = weights[point] * (extinct_ref[where, :] + (2.0 * layer) * diffuse)
                total = term if total is None else total + term
            heat = (1.0 - albedos[half]) * total
            part = pl.ds(half * SUB, SUB)
            heat_ref[level, part, :] = heat
            field = anomaly_ref[level, part, :] + heat
            field_ref[level, part, :] = field
            fields.append(field)
        top_ref[level] = fields[0][:HALO].astype(BF16)
        bottom_ref[level] = fields[-1][SUB - HALO:].astype(BF16)
        return tuple(flux_new)

    lax.fori_loop(0, levels, up, (zero,) * chains)


def rows_of(field_ref, above_ref, below_ref, level):
    halves = field_ref.shape[1] // SUB
    own = [field_ref[level, pl.ds(h * SUB, SUB), :] for h in range(halves)]
    outer = jnp.concatenate(
        [below_ref[level].astype(F32), above_ref[level].astype(F32)], axis=0
    )
    return own + [outer]


def pack_kernel(field_ref, above_ref, below_ref, packed_ref, sent_ref):
    levels, _, width = field_ref.shape
    per_group = width // EDGE
    lanes = lax.broadcasted_iota(jnp.int32, (SUB, width), 1)

    def group_of(group, count):
        packed = None
        for slot in range(count):
            parts = rows_of(field_ref, above_ref, below_ref, group * per_group + slot)
            moved = [pltpu.roll(x, (EDGE * slot + EDGE // 2) % width, 1) for x in parts]
            if packed is None:
                packed = moved
            else:
                packed = [jnp.where(lanes >= EDGE * slot, m, p) for m, p in zip(moved, packed)]
        for part, value in enumerate(packed):
            packed_ref[group, pl.ds(part * SUB, SUB), :] = value
            sent_ref[group, pl.ds(part * SUB, SUB), :] = value.astype(BF16)

    full = levels // per_group
    lax.fori_loop(0, full, lambda g, c: (group_of(g, per_group), c)[1], 0)
    if levels % per_group:
        group_of(full, levels % per_group)


def around(parts, first, final):
    down = [pltpu.roll(x, 1, 0) for x in parts]
    up = [pltpu.roll(x, SUB - 1, 0) for x in parts]
    count = len(parts)
    return [
        jnp.where(first, down[i - 1], down[i]) + jnp.where(final, up[(i + 1) % count], up[i])
        for i in range(count)
    ]


def inside(keep_ref, width):
    sub = lax.broadcasted_iota(jnp.int32, (SUB, width), 0)
    keep = jnp.where(sub < HALO, keep_ref[1], keep_ref[0]).astype(F32)
    return sub == 0, sub == SUB - 1, keep


def main_kernel(keep_ref, field_ref, above_ref, below_ref, out_ref):
    levels, _, width = field_ref.shape
    first, final, keep = inside(keep_ref, width)

    def one_level(level, carry):
        parts = rows_of(field_ref, above_ref, below_ref, level)
        for _ in range(DIFF_STEPS):
            vertical = around(parts, first, final)
            parts = [
                x + v + (pltpu.roll(x, 1, 1) + pltpu.roll(x, width - 1, 1))
                for x, v in zip(parts, vertical)
            ]
            parts[-1] = parts[-1] * keep
        for half, value in enumerate(parts[:-1]):
            out_ref[level, pl.ds(half * SUB, SUB), :] = value * step_scale
        return carry

    lax.fori_loop(0, levels, one_level, 0)


def edge_kernel(keep_ref, packed_ref, west_ref, east_ref, main_ref, out_ref):
    levels, rows, width = main_ref.shape
    per_group = width // EDGE
    halves = rows // SUB
    first, final, keep = inside(keep_ref, width)
    lanes = lax.broadcasted_iota(jnp.int32, (SUB, width), 1)
    column = lanes % EDGE
    mid = EDGE // 2
    last_own = column == mid - 1
    first_own = column == mid
    touched = (lanes < HALO) | (lanes >= width - HALO)

    def group_of(group, count):
        own, other = [], []
        for part in range(halves + 1):
            where = pl.ds(part * SUB, SUB)
            own.append(packed_ref[group, where, :])
            other.append(
                jnp.where(
                    column < mid,
                    west_ref[group, where, :].astype(F32),
                    east_ref[group, where, :].astype(F32),
                )
            )
        for _ in range(DIFF_STEPS):
            own_rows = around(own, first, final)
            other_rows = around(other, first, final)
            own_new, other_new = [], []
            for x, y, v, u in zip(own, other, own_rows, other_rows):
                xe, ye = pltpu.roll(x, width - 1, 1), pltpu.roll(y, width - 1, 1)
                xw, yw = pltpu.roll(x, 1, 1), pltpu.roll(y, 1, 1)
                own_new.append(
                    x + v + (jnp.where(first_own, yw, xw) + jnp.where(last_own, ye, xe))
                )
                other_new.append(
                    y + u + (jnp.where(first_own, xw, yw) + jnp.where(last_own, xe, ye))
                )
            own, other = own_new, other_new
            own[-1] = own[-1] * keep
            other[-1] = other[-1] * keep
        for half in range(halves):
            scaled = own[half] * step_scale
            for slot in range(count):
                moved = pltpu.roll(scaled, (width - EDGE * slot - mid) % width, 1)
                level = group * per_group + slot
                where = pl.ds(half * SUB, SUB)
                out_ref[level, where, :] = jnp.where(touched, moved, main_ref[level, where, :])

    full = levels // per_group
    lax.fori_loop(0, full, lambda g, c: (group_of(g, per_group), c)[1], 0)
    if levels % per_group:
        group_of(full, levels % per_group)


def per_device(optical_depth, albedo, insolation, sunlit, point_weight, anomaly):
    rows, levels, points, width = optical_depth.shape
    planes = jax.ShapeDtypeStruct((levels, rows, width), F32)
    edges = jax.ShapeDtypeStruct((levels, HALO, width), BF16)
    sweep = pltpu.VMEM((levels * rows * points, width), F32)
    heat, field, top, bottom = pl.pallas_call(
        radiate_kernel,
        in_specs=[smem(), smem(), vmem(), vmem(), vmem(), vmem()],
        out_specs=[vmem()] * 4,
        out_shape=[planes, planes, edges, edges],
        scratch_shapes=[sweep] * 4,
        name="radiate",
    )(
        point_weight, sunlit.reshape(rows), optical_depth, jnp.swapaxes(albedo, 0, 1), insolation,
        jnp.swapaxes(anomaly, 0, 1),
    )
    tiles = lax.axis_size("tiles")
    here = lax.axis_index("tiles")
    down = [(i, i + 1) for i in range(tiles - 1)]
    above = lax.ppermute(bottom, "tiles", down)
    below = lax.ppermute(top, "tiles", [(j, i) for i, j in down])
    keep = jnp.stack([here > 0, here < tiles - 1]).astype(jnp.int32)
    groups = -(-levels * EDGE // width)
    side = (groups, rows + SUB, width)
    packed, sent = pl.pallas_call(
        pack_kernel,
        in_specs=[vmem()] * 3,
        out_specs=[vmem()] * 2,
        out_shape=[jax.ShapeDtypeStruct(side, F32), jax.ShapeDtypeStruct(side, BF16)],
        name="pack",
    )(field, above, below)
    bands = lax.axis_size("band")
    east = [(i, (i + 1) % bands) for i in range(bands)]
    from_west = lax.ppermute(sent, "band", east)
    from_east = lax.ppermute(sent, "band", [(j, i) for i, j in east])
    inner = pl.pallas_call(
        main_kernel,
        in_specs=[smem()] + [vmem()] * 3,
        out_specs=vmem(),
        out_shape=planes,
        name="inner",
    )(keep, field, above, below)
    smoothed = pl.pallas_call(
        edge_kernel,
        in_specs=[smem()] + [vmem()] * 4,
        out_specs=vmem(),
        out_shape=planes,
        input_output_aliases={4: 0},
        name="edge",
    )(keep, packed, from_west, from_east, inner)
    return jnp.swapaxes(heat, 0, 1), jnp.swapaxes(smoothed, 0, 1)


def solution(mesh):
    placed = (
        P("tiles", None, None, "band"),
        P("tiles", None, "band"),
        P("tiles", "band"),
        P("tiles", "band"),
        P(),
        P("tiles", None, "band"),
    )
    return jax.shard_map(
        per_device,
        mesh=mesh,
        in_specs=placed,
        out_specs=(P("tiles", None, "band"), P("tiles", None, "band")),
        check_vma=False,
    )
```

```python
import jax
import jax.numpy as jnp
from jax import lax
from jax.experimental import pallas as pl
from jax.experimental.pallas import tpu as pltpu
from jax.sharding import PartitionSpec as P

DIFF_STEPS = 4
BATCH = 10
GROUPS = 4
HALO = 4
EDGE = 16
SUB = 8
F32 = jnp.float32
BF16 = jnp.bfloat16
base_loss = 0.005
step_scale = 0.2**DIFF_STEPS


def vmem():
    return pl.BlockSpec(memory_space=pltpu.VMEM)


def smem():
    return pl.BlockSpec(memory_space=pltpu.SMEM)


def radiate_kernel(
    weight_ref, lit_ref, depth_ref, albedo_ref, sun_ref, anomaly_ref,
    heat_ref, field_ref, top_ref, bottom_ref,
    spread_ref, ratio_ref, swept_ref, extinct_ref,
):
    rows, levels, points, width = depth_ref.shape
    per_level = rows * points
    halves = rows // SUB
    chains = halves * points
    sun = sun_ref[...].astype(F32)
    row_ids = lax.broadcasted_iota(jnp.int32, (rows, width), 0)
    lit = jnp.zeros((rows, width), jnp.int32)
    for row in range(rows):
        lit = jnp.where(row_ids == row, lit_ref[row], lit)
    sun = jnp.where(lit == 1, sun, 0.0)
    suns = [sun[h * SUB:(h + 1) * SUB] for h in range(halves)]

    def spread(level):
        for row in range(rows):
            spread_ref[pl.ds(level * per_level + points * row, points), :] = (
                depth_ref[row, level].astype(F32)
            )

    def depth_of(level, half, point):
        start = level * per_level + half * SUB * points + point
        return spread_ref[pl.ds(start, SUB, stride=points), :]

    def albedo_of(level):
        both = albedo_ref[level].astype(F32)
        return [both[h * SUB:(h + 1) * SUB] for h in range(halves)]

    def place(level, chain):
        return pl.ds(pl.multiple_of(level * per_level + chain * SUB, SUB), SUB)

    zero = jnp.zeros((SUB, width), F32)
    one = jnp.ones((SUB, width), F32)

    def down(level, carry):
        link_prev, albedo_now, depth, light, ratio, swept = carry
        last = level == levels - 1
        following = jnp.where(last, level, level + 1)
        spread(following)
        albedo_next = albedo_of(following)
        out = ([], [], [], [], [])
        for half in range(halves):
            albedo = albedo_now[half]
            before = link_prev[half]
            link = jnp.where(last, 0.0, albedo * albedo_next[half])
            slope = 2.0 * (1.0 - albedo)
            level_part = base_loss + before + link
            for point in range(points):
                chain = half * points + point
                layer = depth_of(level, half, point)
                depth_new = depth[chain] + layer
                light_new = jnp.exp(depth_new * -2.0)
                extinct = suns[half] * (light[chain] - light_new)
                inverse = 1.0 / (level_part + slope * layer - before * ratio[chain])
                ratio_new = link * inverse
                swept_new = (albedo * extinct + before * swept[chain]) * inverse
                where = place(level, chain)
                ratio_ref[where, :] = ratio_new
                swept_ref[where, :] = swept_new
                extinct_ref[where, :] = extinct
                for item, value in zip(out, (depth_new, light_new, ratio_new, swept_new)):
                    item.append(value)
            out[4].append(link)
        return (
            tuple(out[4]), tuple(albedo_next), tuple(out[0]), tuple(out[1]), tuple(out[2]),
            tuple(out[3]),
        )

    spread(0)
    lax.fori_loop(
        0, levels, down,
        ((zero,) * halves, tuple(albedo_of(0)), (zero,) * chains, (one,) * chains,
         (zero,) * chains, (zero,) * chains),
    )
    weights = [weight_ref[point] for point in range(points)]

    def up(i, flux):
        level = levels - 1 - i
        albedos = albedo_of(level)
        flux_new = []
        fields = []
        for half in range(halves):
            total = None
            for point in range(points):
                chain = half * points + point
                where = place(level, chain)
                diffuse = swept_ref[where, :] + ratio_ref[where, :] * flux[chain]
                flux_new.append(diffuse)
                layer = depth_of(level, half, point)
                term = weights[point] * (extinct_ref[where, :] + (2.0 * layer) * diffuse)
                total = term if total is None else total + term
            heat = (1.0 - albedos[half]) * total
            part = pl.ds(half * SUB, SUB)
            heat_ref[level, part, :] = heat
            field = anomaly_ref[level, part, :] + heat
            field_ref[level, part, :] = field
            fields.append(field)
        top_ref[level] = fields[0][:HALO].astype(BF16)
        bottom_ref[level] = fields[-1][SUB - HALO:].astype(BF16)
        return tuple(flux_new)

    lax.fori_loop(0, levels, up, (zero,) * chains)


def rows_of(field_ref, above_ref, below_ref, level):
    halves = field_ref.shape[1] // SUB
    own = [field_ref[level, pl.ds(h * SUB, SUB), :] for h in range(halves)]
    outer = jnp.concatenate(
        [below_ref[level].astype(F32), above_ref[level].astype(F32)], axis=0
    )
    return own + [outer]


def pack_kernel(field_ref, above_ref, below_ref, packed_ref, sent_ref):
    levels, _, width = field_ref.shape
    per_group = width // EDGE
    lanes = lax.broadcasted_iota(jnp.int32, (SUB, width), 1)

    def group_of(group, count):
        packed = None
        for slot in range(count):
            parts = rows_of(field_ref, above_ref, below_ref, group * per_group + slot)
            moved = [pltpu.roll(x, (EDGE * slot + EDGE // 2) % width, 1) for x in parts]
            if packed is None:
                packed = moved
            else:
                packed = [jnp.where(lanes >= EDGE * slot, m, p) for m, p in zip(moved, packed)]
        for part, value in enumerate(packed):
            packed_ref[group, pl.ds(part * SUB, SUB), :] = value
            sent_ref[group, pl.ds(part * SUB, SUB), :] = value.astype(BF16)

    full = levels // per_group
    lax.fori_loop(0, full, lambda g, c: (group_of(g, per_group), c)[1], 0)
    if levels % per_group:
        group_of(full, levels % per_group)


def around(parts, first, final):
    down = [pltpu.roll(x, 1, 0) for x in parts]
    up = [pltpu.roll(x, SUB - 1, 0) for x in parts]
    count = len(parts)
    return [
        jnp.where(first, down[i - 1], down[i]) + jnp.where(final, up[(i + 1) % count], up[i])
        for i in range(count)
    ]


def inside(keep_ref, width):
    sub = lax.broadcasted_iota(jnp.int32, (SUB, width), 0)
    keep = jnp.where(sub < HALO, keep_ref[1], keep_ref[0]).astype(F32)
    return sub == 0, sub == SUB - 1, keep


def main_kernel(keep_ref, field_ref, above_ref, below_ref, out_ref):
    levels, _, width = field_ref.shape
    first, final, keep = inside(keep_ref, width)

    def some_levels(block, carry):
        found = [block * BATCH + i for i in range(BATCH)]
        sets = [rows_of(field_ref, above_ref, below_ref, level) for level in found]
        for _ in range(DIFF_STEPS):
            new = []
            for parts in sets:
                vertical = around(parts, first, final)
                parts = [
                    x + v + (pltpu.roll(x, 1, 1) + pltpu.roll(x, width - 1, 1))
                    for x, v in zip(parts, vertical)
                ]
                parts[-1] = parts[-1] * keep
                new.append(parts)
            sets = new
        for level, parts in zip(found, sets):
            for half, value in enumerate(parts[:-1]):
                out_ref[level, pl.ds(half * SUB, SUB), :] = value * step_scale
        return carry

    lax.fori_loop(0, levels // BATCH, some_levels, 0)


def edge_kernel(keep_ref, packed_ref, west_ref, east_ref, main_ref, out_ref):
    levels, rows, width = main_ref.shape
    per_group = width // EDGE
    halves = rows // SUB
    first, final, keep = inside(keep_ref, width)
    lanes = lax.broadcasted_iota(jnp.int32, (SUB, width), 1)
    column = lanes % EDGE
    mid = EDGE // 2
    last_own = column == mid - 1
    first_own = column == mid
    touched = (lanes < HALO) | (lanes >= width - HALO)

    def block_of(block, counts):
        groups = [block * GROUPS + i for i in range(len(counts))]
        sets = []
        for group in groups:
            own, other = [], []
            for part in range(halves + 1):
                where = pl.ds(part * SUB, SUB)
                own.append(packed_ref[group, where, :])
                other.append(
                    jnp.where(
                        column < mid,
                        west_ref[group, where, :].astype(F32),
                        east_ref[group, where, :].astype(F32),
                    )
                )
            sets.append((own, other))
        for _ in range(DIFF_STEPS):
            new = []
            for own, other in sets:
                own_rows = around(own, first, final)
                other_rows = around(other, first, final)
                own_new, other_new = [], []
                for x, y, v, u in zip(own, other, own_rows, other_rows):
                    xe, ye = pltpu.roll(x, width - 1, 1), pltpu.roll(y, width - 1, 1)
                    xw, yw = pltpu.roll(x, 1, 1), pltpu.roll(y, 1, 1)
                    own_new.append(
                        x + v + (jnp.where(first_own, yw, xw) + jnp.where(last_own, ye, xe))
                    )
                    other_new.append(
                        y + u + (jnp.where(first_own, xw, yw) + jnp.where(last_own, xe, ye))
                    )
                own_new[-1] = own_new[-1] * keep
                other_new[-1] = other_new[-1] * keep
                new.append((own_new, other_new))
            sets = new
        for group, count, (own, _) in zip(groups, counts, sets):
            for half in range(halves):
                scaled = own[half] * step_scale
                where = pl.ds(half * SUB, SUB)
                for slot in range(count):
                    moved = pltpu.roll(scaled, (width - EDGE * slot - mid) % width, 1)
                    level = group * per_group + slot
                    out_ref[level, where, :] = jnp.where(
                        touched, moved, main_ref[level, where, :]
                    )

    full = levels // per_group
    counts = [per_group] * full + ([levels % per_group] if levels % per_group else [])
    blocks = full // GROUPS
    lax.fori_loop(0, blocks, lambda b, c: (block_of(b, counts[:GROUPS]), c)[1], 0)
    if counts[blocks * GROUPS:]:
        block_of(blocks, counts[blocks * GROUPS:])


def per_device(optical_depth, albedo, insolation, sunlit, point_weight, anomaly):
    rows, levels, points, width = optical_depth.shape
    planes = jax.ShapeDtypeStruct((levels, rows, width), F32)
    edges = jax.ShapeDtypeStruct((levels, HALO, width), BF16)
    sweep = pltpu.VMEM((levels * rows * points, width), F32)
    heat, field, top, bottom = pl.pallas_call(
        radiate_kernel,
        in_specs=[smem(), smem(), vmem(), vmem(), vmem(), vmem()],
        out_specs=[vmem()] * 4,
        out_shape=[planes, planes, edges, edges],
        scratch_shapes=[sweep] * 4,
        name="radiate",
    )(
        point_weight, sunlit.reshape(rows), optical_depth, jnp.swapaxes(albedo, 0, 1), insolation,
        jnp.swapaxes(anomaly, 0, 1),
    )
    tiles = lax.axis_size("tiles")
    here = lax.axis_index("tiles")
    down = [(i, i + 1) for i in range(tiles - 1)]
    above = lax.ppermute(bottom, "tiles", down)
    below = lax.ppermute(top, "tiles", [(j, i) for i, j in down])
    keep = jnp.stack([here > 0, here < tiles - 1]).astype(jnp.int32)
    groups = -(-levels * EDGE // width)
    side = (groups, rows + SUB, width)
    packed, sent = pl.pallas_call(
        pack_kernel,
        in_specs=[vmem()] * 3,
        out_specs=[vmem()] * 2,
        out_shape=[jax.ShapeDtypeStruct(side, F32), jax.ShapeDtypeStruct(side, BF16)],
        name="pack",
    )(field, above, below)
    bands = lax.axis_size("band")
    east = [(i, (i + 1) % bands) for i in range(bands)]
    from_west = lax.ppermute(sent, "band", east)
    from_east = lax.ppermute(sent, "band", [(j, i) for i, j in east])
    inner = pl.pallas_call(
        main_kernel,
        in_specs=[smem()] + [vmem()] * 3,
        out_specs=vmem(),
        out_shape=planes,
        name="inner",
    )(keep, field, above, below)
    smoothed = pl.pallas_call(
        edge_kernel,
        in_specs=[smem()] + [vmem()] * 4,
        out_specs=vmem(),
        out_shape=planes,
        input_output_aliases={4: 0},
        name="edge",
    )(keep, packed, from_west, from_east, inner)
    return jnp.swapaxes(heat, 0, 1), jnp.swapaxes(smoothed, 0, 1)


def solution(mesh):
    placed = (
        P("tiles", None, None, "band"),
        P("tiles", None, "band"),
        P("tiles", "band"),
        P("tiles", "band"),
        P(),
        P("tiles", None, "band"),
    )
    return jax.shard_map(
        per_device,
        mesh=mesh,
        in_specs=placed,
        out_specs=(P("tiles", None, "band"), P("tiles", None, "band")),
        check_vma=False,
    )
```

```python
import functools
import math

import jax
import jax.numpy as jnp
from jax import lax
from jax.experimental import pallas as pl
from jax.experimental.pallas import tpu as pltpu
from jax.sharding import PartitionSpec as P

DIFF_STEPS = 4
BATCH = 10
GROUPS = 4
UNROLL_DOWN = 3
UNROLL_UP = 6
LIGHT_RATE = -2.0 * math.log2(math.e)
HALO = 4
EDGE = 16
SUB = 8
F32 = jnp.float32
BF16 = jnp.bfloat16
base_loss = 0.005
step_scale = 0.2**DIFF_STEPS


def vmem():
    return pl.BlockSpec(memory_space=pltpu.VMEM)


def smem():
    return pl.BlockSpec(memory_space=pltpu.SMEM)


def radiate_kernel(
    here_ref, weight_ref, lit_ref, depth_ref, albedo_ref, sun_ref, anomaly_ref,
    heat_ref, field_ref, pair_ref, step_ref,
    spread_ref, ratio_ref, swept_ref, extinct_ref,
):
    rows, levels, points, width = depth_ref.shape
    per_level = rows * points
    halves = rows // SUB
    chains = halves * points
    sun = sun_ref[...].astype(F32)
    row_ids = lax.broadcasted_iota(jnp.int32, (rows, width), 0)
    lit = jnp.zeros((rows, width), jnp.int32)
    for row in range(rows):
        lit = jnp.where(row_ids == row, lit_ref[row], lit)
    sun = jnp.where(lit == 1, sun, 0.0)
    suns = [sun[h * SUB:(h + 1) * SUB] for h in range(halves)]

    def spread(level):
        for row in range(rows):
            spread_ref[pl.ds(level * per_level + points * row, points), :] = (
                depth_ref[row, level].astype(F32)
            )

    def depth_of(level, half, point):
        start = level * per_level + half * SUB * points + point
        return spread_ref[pl.ds(start, SUB, stride=points), :]

    def albedo_of(level):
        both = albedo_ref[level].astype(F32)
        return [both[h * SUB:(h + 1) * SUB] for h in range(halves)]

    def place(level, chain):
        return pl.ds(pl.multiple_of(level * per_level + chain * SUB, SUB), SUB)

    zero = jnp.zeros((SUB, width), F32)
    one = jnp.ones((SUB, width), F32)

    def down(level, carry):
        link_prev, albedo_now, depth, light, ratio, swept = carry
        last = level == levels - 1
        following = jnp.where(last, level, level + 1)
        spread(following)
        albedo_next = albedo_of(following)
        out = ([], [], [], [], [])
        for half in range(halves):
            albedo = albedo_now[half]
            before = link_prev[half]
            link = jnp.where(last, 0.0, albedo * albedo_next[half])
            slope = 2.0 * (1.0 - albedo)
            level_part = base_loss + before + link
            for point in range(points):
                chain = half * points + point
                layer = depth_of(level, half, point)
                depth_new = depth[chain] + layer
                light_new = jnp.exp2(depth_new * LIGHT_RATE)
                extinct = suns[half] * (light[chain] - light_new)
                inverse = 1.0 / (level_part + slope * layer - before * ratio[chain])
                ratio_new = link * inverse
                swept_new = (albedo * extinct + before * swept[chain]) * inverse
                where = place(level, chain)
                ratio_ref[where, :] = ratio_new
                swept_ref[where, :] = swept_new
                extinct_ref[where, :] = extinct
                for item, value in zip(out, (depth_new, light_new, ratio_new, swept_new)):
                    item.append(value)
            out[4].append(link)
        return (
            tuple(out[4]), tuple(albedo_next), tuple(out[0]), tuple(out[1]), tuple(out[2]),
            tuple(out[3]),
        )

    spread(0)
    lax.fori_loop(
        0, levels, down,
        ((zero,) * halves, tuple(albedo_of(0)), (zero,) * chains, (one,) * chains,
         (zero,) * chains, (zero,) * chains),
        unroll=UNROLL_DOWN,
    )
    even = here_ref[0] % 2 == 0
    weights = [weight_ref[point] for point in range(points)]

    def up(i, flux):
        level = levels - 1 - i
        albedos = albedo_of(level)
        flux_new = []
        fields = []
        for half in range(halves):
            total = None
            for point in range(points):
                chain = half * points + point
                where = place(level, chain)
                diffuse = swept_ref[where, :] + ratio_ref[where, :] * flux[chain]
                flux_new.append(diffuse)
                layer = depth_of(level, half, point)
                term = weights[point] * (extinct_ref[where, :] + (2.0 * layer) * diffuse)
                total = term if total is None else total + term
            heat = (1.0 - albedos[half]) * total
            part = pl.ds(half * SUB, SUB)
            heat_ref[level, part, :] = heat
            field = anomaly_ref[level, part, :] + heat
            field_ref[level, part, :] = field
            fields.append(field)
        top, bottom = fields[0][:HALO], fields[-1][SUB - HALO:]
        pair_ref[level] = jnp.where(even, bottom, top).astype(BF16)
        step_ref[level] = jnp.where(even, top, bottom).astype(BF16)
        return tuple(flux_new)

    lax.fori_loop(0, levels, up, (zero,) * chains, unroll=UNROLL_UP)


def outer_rows(here_ref, pair_ref, step_ref, level):
    pair, step = pair_ref[level].astype(F32), step_ref[level].astype(F32)
    even = here_ref[0] % 2 == 0
    below = jnp.where(even, pair, step)
    above = jnp.where(even, step, pair)
    return jnp.concatenate([below, above], axis=0)


def pack_levels(lanes, parts):
    width = lanes.shape[1]
    packed = None
    for slot, part in enumerate(parts):
        moved = pltpu.roll(part, (EDGE * slot + EDGE // 2) % width, 1)
        packed = moved if packed is None else jnp.where(lanes >= EDGE * slot, moved, packed)
    return packed


def each_block(levels, per_group, body):
    full = levels // per_group
    counts = [per_group] * full + ([levels % per_group] if levels % per_group else [])
    blocks = full // GROUPS
    lax.fori_loop(0, blocks, lambda b, c: (body(b, counts[:GROUPS]), c)[1], 0)
    if counts[blocks * GROUPS:]:
        body(blocks, counts[blocks * GROUPS:])


def pack_own_kernel(field_ref, packed_ref):
    levels, rows, width = field_ref.shape
    per_group = width // EDGE
    lanes = lax.broadcasted_iota(jnp.int32, (SUB, width), 1)

    def block_of(block, counts):
        for i, count in enumerate(counts):
            group = block * GROUPS + i
            for half in range(rows // SUB):
                where = pl.ds(half * SUB, SUB)
                packed_ref[group, where, :] = pack_levels(
                    lanes, [field_ref[group * per_group + k, where, :] for k in range(count)]
                )

    each_block(levels, per_group, block_of)


def pack_outer_kernel(here_ref, pair_ref, step_ref, own_ref, outer_ref, sent_ref):
    levels, _, width = pair_ref.shape
    rows = own_ref.shape[1]
    per_group = width // EDGE
    lanes = lax.broadcasted_iota(jnp.int32, (SUB, width), 1)

    def block_of(block, counts):
        for i, count in enumerate(counts):
            group = block * GROUPS + i
            packed = pack_levels(
                lanes,
                [outer_rows(here_ref, pair_ref, step_ref, group * per_group + k)
                 for k in range(count)],
            )
            outer_ref[group] = packed
            sent_ref[group, pl.ds(rows, SUB), :] = packed.astype(BF16)
            sent_ref[group, pl.ds(0, rows), :] = own_ref[group].astype(BF16)

    each_block(levels, per_group, block_of)


def around(parts, first, final):
    down = [pltpu.roll(x, 1, 0) for x in parts]
    up = [pltpu.roll(x, SUB - 1, 0) for x in parts]
    count = len(parts)
    return [
        jnp.where(first, down[i - 1], down[i]) + jnp.where(final, up[(i + 1) % count], up[i])
        for i in range(count)
    ]


def inside(here_ref, tiles, width):
    sub = lax.broadcasted_iota(jnp.int32, (SUB, width), 0)
    tile = here_ref[0]
    keep = jnp.where(
        sub < HALO, (tile < tiles - 1).astype(jnp.int32), (tile > 0).astype(jnp.int32)
    )
    return sub == 0, sub == SUB - 1, keep.astype(F32)


def main_kernel(tiles, here_ref, field_ref, pair_ref, step_ref, out_ref):
    levels, rows, width = field_ref.shape
    first, final, keep = inside(here_ref, tiles, width)

    def some_levels(block, carry):
        found = [block * BATCH + i for i in range(BATCH)]
        sets = [
            [field_ref[level, pl.ds(h * SUB, SUB), :] for h in range(rows // SUB)]
            + [outer_rows(here_ref, pair_ref, step_ref, level)]
            for level in found
        ]
        for _ in range(DIFF_STEPS):
            new = []
            for parts in sets:
                vertical = around(parts, first, final)
                parts = [
                    x + v + (pltpu.roll(x, 1, 1) + pltpu.roll(x, width - 1, 1))
                    for x, v in zip(parts, vertical)
                ]
                parts[-1] = parts[-1] * keep
                new.append(parts)
            sets = new
        for level, parts in zip(found, sets):
            for half, value in enumerate(parts[:-1]):
                out_ref[level, pl.ds(half * SUB, SUB), :] = value * step_scale
        return carry

    lax.fori_loop(0, levels // BATCH, some_levels, 0)


def edge_kernel(
    tiles, here_ref, side_ref, own_ref, outer_ref, near_ref, far_ref, main_ref, out_ref
):
    levels, rows, width = main_ref.shape
    per_group = width // EDGE
    halves = rows // SUB
    first, final, keep = inside(here_ref, tiles, width)
    swapped = side_ref[0] % 2 == 1
    lanes = lax.broadcasted_iota(jnp.int32, (SUB, width), 1)
    column = lanes % EDGE
    mid = EDGE // 2
    last_own = column == mid - 1
    first_own = column == mid
    from_near = (column < mid).astype(jnp.int32) == swapped.astype(jnp.int32)
    touched = (lanes < HALO) | (lanes >= width - HALO)

    def block_of(block, counts):
        groups = [block * GROUPS + i for i in range(len(counts))]
        sets = []
        for group in groups:
            own, other = [], []
            for part in range(halves + 1):
                where = pl.ds(part * SUB, SUB)
                own.append(own_ref[group, where, :] if part < halves else outer_ref[group])
                near = near_ref[group, where, :].astype(F32)
                far = far_ref[group, where, :].astype(F32)
                other.append(jnp.where(from_near, near, far))
            sets.append((own, other))
        for _ in range(DIFF_STEPS):
            new = []
            for own, other in sets:
                own_rows = around(own, first, final)
                other_rows = around(other, first, final)
                own_new, other_new = [], []
                for x, y, v, u in zip(own, other, own_rows, other_rows):
                    xe, ye = pltpu.roll(x, width - 1, 1), pltpu.roll(y, width - 1, 1)
                    xw, yw = pltpu.roll(x, 1, 1), pltpu.roll(y, 1, 1)
                    own_new.append(
                        x + v + (jnp.where(first_own, yw, xw) + jnp.where(last_own, ye, xe))
                    )
                    other_new.append(
                        y + u + (jnp.where(first_own, xw, yw) + jnp.where(last_own, xe, ye))
                    )
                own_new[-1] = own_new[-1] * keep
                other_new[-1] = other_new[-1] * keep
                new.append((own_new, other_new))
            sets = new
        for group, count, (own, _) in zip(groups, counts, sets):
            for half in range(halves):
                scaled = own[half] * step_scale
                where = pl.ds(half * SUB, SUB)
                for slot in range(count):
                    moved = pltpu.roll(scaled, (width - EDGE * slot - mid) % width, 1)
                    level = group * per_group + slot
                    out_ref[level, where, :] = jnp.where(
                        touched, moved, main_ref[level, where, :]
                    )

    each_block(levels, per_group, block_of)


def fast(shape, dtype):
    return pltpu.VMEM(shape, dtype)


def held(x):
    return pltpu.with_memory_space_constraint(x, pltpu.VMEM)


def swaps(size, first, ring):
    ends = range(first, size if ring else size - 1, 2)
    return [pair for i in ends for pair in ((i, (i + 1) % size), ((i + 1) % size, i))]


def per_device(optical_depth, albedo, insolation, sunlit, point_weight, anomaly):
    rows, levels, points, width = optical_depth.shape
    tiles, bands = lax.axis_size("tiles"), lax.axis_size("band")
    here = lax.axis_index("tiles").astype(jnp.int32).reshape(1)
    side = lax.axis_index("band").astype(jnp.int32).reshape(1)
    planes = (levels, rows, width)
    edges = (levels, HALO, width)
    groups = -(-levels * EDGE // width)
    sweep = pltpu.VMEM((levels * rows * points, width), F32)
    heat, field, pair_edge, step_edge = pl.pallas_call(
        radiate_kernel,
        in_specs=[smem(), smem(), smem(), vmem(), vmem(), vmem(), vmem()],
        out_specs=[vmem()] * 4,
        out_shape=[
            jax.ShapeDtypeStruct(planes, F32), fast(planes, F32), fast(edges, BF16),
            fast(edges, BF16),
        ],
        scratch_shapes=[sweep] * 4,
        name="radiate",
    )(
        here, point_weight, sunlit.reshape(rows), optical_depth, jnp.swapaxes(albedo, 0, 1),
        insolation, jnp.swapaxes(anomaly, 0, 1),
    )
    from_pair = lax.ppermute(pair_edge, "tiles", swaps(tiles, 0, False))
    from_step = lax.ppermute(step_edge, "tiles", swaps(tiles, 1, False))
    own = pl.pallas_call(
        pack_own_kernel,
        in_specs=[vmem()],
        out_specs=vmem(),
        out_shape=fast((groups, rows, width), F32),
        name="pack_own",
    )(held(field))
    outer, sent = pl.pallas_call(
        pack_outer_kernel,
        in_specs=[smem()] + [vmem()] * 3,
        out_specs=[vmem()] * 2,
        out_shape=[fast((groups, SUB, width), F32), fast((groups, rows + SUB, width), BF16)],
        name="pack_outer",
    )(here, held(from_pair), held(from_step), held(own))
    near = lax.ppermute(sent, "band", swaps(bands, 0, True))
    far = lax.ppermute(sent, "band", swaps(bands, 1, True))
    inner = pl.pallas_call(
        functools.partial(main_kernel, tiles),
        in_specs=[smem()] + [vmem()] * 3,
        out_specs=vmem(),
        out_shape=fast(planes, F32),
        name="inner",
    )(here, held(field), held(from_pair), held(from_step))
    smoothed = pl.pallas_call(
        functools.partial(edge_kernel, tiles),
        in_specs=[smem(), smem()] + [vmem()] * 5,
        out_specs=vmem(),
        out_shape=jax.ShapeDtypeStruct(planes, F32),
        name="edge",
    )(here, side, held(own), held(outer), held(near), held(far), held(inner))
    return jnp.swapaxes(heat, 0, 1), jnp.swapaxes(smoothed, 0, 1)


def solution(mesh):
    placed = (
        P("tiles", None, None, "band"),
        P("tiles", None, "band"),
        P("tiles", "band"),
        P("tiles", "band"),
        P(),
        P("tiles", None, "band"),
    )
    return jax.shard_map(
        per_device,
        mesh=mesh,
        in_specs=placed,
        out_specs=(P("tiles", None, "band"), P("tiles", None, "band")),
        check_vma=False,
    )
```

```python
import functools
import math

import jax
import jax.numpy as jnp
from jax import lax
from jax.experimental import pallas as pl
from jax.experimental.pallas import tpu as pltpu
from jax.sharding import PartitionSpec as P

DIFF_STEPS = 4
BATCH = 10
GROUPS = 4
CHUNK = 15
UNROLL_DOWN = 5
UNROLL_UP = 5
LIGHT_RATE = -2.0 * math.log2(math.e)
HALO = 4
EDGE = 16
SUB = 8
F32 = jnp.float32
BF16 = jnp.bfloat16
base_loss = 0.005
step_scale = 0.2**DIFF_STEPS


def vmem():
    return pl.BlockSpec(memory_space=pltpu.VMEM)


def whole():
    return pl.BlockSpec(memory_space=pl.ANY)


def smem():
    return pl.BlockSpec(memory_space=pltpu.SMEM)


def radiate_kernel(
    here_ref, weight_ref, lit_ref, depth_hbm, albedo_hbm, sun_ref, anomaly_hbm,
    heat_hbm, field_ref, pair_ref, step_ref,
    spread_ref, ratio_ref, swept_ref, extinct_ref,
    depth_ref, albedo_ref, anomaly_ref, heat_ref, depth_sems, other_sems, heat_sems,
):
    rows, levels, points, width = depth_ref.shape
    chunks = levels // CHUNK

    def depth_copy(chunk):
        part = pl.ds(chunk * CHUNK, CHUNK)
        return pltpu.make_async_copy(
            depth_hbm.at[:, part], depth_ref.at[:, part], depth_sems.at[chunk]
        )

    def heat_copy(chunk):
        part = pl.ds(chunk * CHUNK, CHUNK)
        return pltpu.make_async_copy(
            heat_ref.at[part], heat_hbm.at[part], heat_sems.at[chunk]
        )

    albedo_copy = pltpu.make_async_copy(albedo_hbm, albedo_ref, other_sems.at[0])
    anomaly_copy = pltpu.make_async_copy(anomaly_hbm, anomaly_ref, other_sems.at[1])
    depth_copy(0).start()
    albedo_copy.start()
    for chunk in range(1, chunks):
        depth_copy(chunk).start()
    anomaly_copy.start()
    per_level = rows * points
    halves = rows // SUB
    chains = halves * points
    sun = sun_ref[...].astype(F32)
    row_ids = lax.broadcasted_iota(jnp.int32, (rows, width), 0)
    lit = jnp.zeros((rows, width), jnp.int32)
    for row in range(rows):
        lit = jnp.where(row_ids == row, lit_ref[row], lit)
    sun = jnp.where(lit == 1, sun, 0.0)
    suns = [sun[h * SUB:(h + 1) * SUB] for h in range(halves)]
    weights = [weight_ref[point] for point in range(points)]

    def spread(level):
        for row in range(rows):
            spread_ref[pl.ds(level * per_level + points * row, points), :] = (
                depth_ref[row, level].astype(F32)
            )

    def depth_of(level, half, point):
        start = level * per_level + half * SUB * points + point
        return spread_ref[pl.ds(start, SUB, stride=points), :]

    def albedo_of(level):
        both = albedo_ref[level].astype(F32)
        return [both[h * SUB:(h + 1) * SUB] for h in range(halves)]

    def place(level, chain):
        return pl.ds(pl.multiple_of(level * per_level + chain * SUB, SUB), SUB)

    zero = jnp.zeros((SUB, width), F32)
    one = jnp.ones((SUB, width), F32)

    def down(level, carry):
        link_prev, albedo_now, depth, light, ratio, swept = carry
        last = level == levels - 1
        following = jnp.where(last, level, level + 1)
        spread(level)
        albedo_next = albedo_of(following)
        out = ([], [], [], [], [])
        for half in range(halves):
            albedo = albedo_now[half]
            before = link_prev[half]
            link = jnp.where(last, 0.0, albedo * albedo_next[half])
            slope = 2.0 * (1.0 - albedo)
            level_part = base_loss + before + link
            direct = None
            for point in range(points):
                chain = half * points + point
                layer = depth_of(level, half, point)
                depth_new = depth[chain] + layer
                light_new = weights[point] * jnp.exp2(depth_new * LIGHT_RATE)
                extinct = light[chain] - light_new
                direct = extinct if direct is None else direct + extinct
                inverse = 1.0 / (level_part + slope * layer - before * ratio[chain])
                ratio_new = link * inverse
                swept_new = (albedo * extinct + before * swept[chain]) * inverse
                where = place(level, chain)
                ratio_ref[where, :] = ratio_new
                swept_ref[where, :] = swept_new
                for item, value in zip(out, (depth_new, light_new, ratio_new, swept_new)):
                    item.append(value)
            out[4].append(link)
            extinct_ref[level, pl.ds(half * SUB, SUB), :] = direct
        return (
            tuple(out[4]), tuple(albedo_next), tuple(out[0]), tuple(out[1]), tuple(out[2]),
            tuple(out[3]),
        )

    def down_chunk(chunk, carry):
        depth_copy(chunk).wait()
        return lax.fori_loop(
            0, CHUNK, lambda i, c: down(chunk * CHUNK + i, c), carry, unroll=UNROLL_DOWN
        )

    albedo_copy.wait()
    lax.fori_loop(
        0, chunks, down_chunk,
        ((zero,) * halves, tuple(albedo_of(0)), (zero,) * chains,
         tuple(weights[point] * one for _ in range(halves) for point in range(points)),
         (zero,) * chains, (zero,) * chains),
    )
    anomaly_copy.wait()
    even = here_ref[0] % 2 == 0

    def up(level, flux):
        albedos = albedo_of(level)
        flux_new = []
        fields = []
        for half in range(halves):
            total = None
            for point in range(points):
                chain = half * points + point
                where = place(level, chain)
                diffuse = swept_ref[where, :] + ratio_ref[where, :] * flux[chain]
                flux_new.append(diffuse)
                term = depth_of(level, half, point) * diffuse
                total = term if total is None else total + term
            part = pl.ds(half * SUB, SUB)
            absorbed = extinct_ref[level, part, :] + 2.0 * total
            heat = suns[half] * ((1.0 - albedos[half]) * absorbed)
            heat_ref[level, part, :] = heat
            field = anomaly_ref[level, part, :] + heat
            field_ref[level, part, :] = field
            fields.append(field)
        top, bottom = fields[0][:HALO], fields[-1][SUB - HALO:]
        pair_ref[level] = jnp.where(even, bottom, top).astype(BF16)
        step_ref[level] = jnp.where(even, top, bottom).astype(BF16)
        return tuple(flux_new)

    def up_chunk(i, flux):
        chunk = chunks - 1 - i
        last = chunk * CHUNK + CHUNK - 1
        flux = lax.fori_loop(0, CHUNK, lambda k, f: up(last - k, f), flux, unroll=UNROLL_UP)
        heat_copy(chunk).start()
        return flux

    lax.fori_loop(0, chunks, up_chunk, (zero,) * chains)
    for chunk in range(chunks):
        heat_copy(chunk).wait()


def outer_rows(here_ref, pair_ref, step_ref, level):
    pair, step = pair_ref[level].astype(F32), step_ref[level].astype(F32)
    even = here_ref[0] % 2 == 0
    below = jnp.where(even, pair, step)
    above = jnp.where(even, step, pair)
    return jnp.concatenate([below, above], axis=0)


def pack_levels(lanes, parts):
    width = lanes.shape[1]
    packed = None
    for slot, part in enumerate(parts):
        moved = pltpu.roll(part, (EDGE * slot + EDGE // 2) % width, 1)
        packed = moved if packed is None else jnp.where(lanes >= EDGE * slot, moved, packed)
    return packed


def each_block(levels, per_group, body):
    full = levels // per_group
    counts = [per_group] * full + ([levels % per_group] if levels % per_group else [])
    blocks = full // GROUPS
    lax.fori_loop(0, blocks, lambda b, c: (body(b, counts[:GROUPS]), c)[1], 0)
    if counts[blocks * GROUPS:]:
        body(blocks, counts[blocks * GROUPS:])


def pack_own_kernel(field_ref, packed_ref):
    levels, rows, width = field_ref.shape
    per_group = width // EDGE
    lanes = lax.broadcasted_iota(jnp.int32, (SUB, width), 1)

    def block_of(block, counts):
        for i, count in enumerate(counts):
            group = block * GROUPS + i
            for half in range(rows // SUB):
                where = pl.ds(half * SUB, SUB)
                packed_ref[group, where, :] = pack_levels(
                    lanes, [field_ref[group * per_group + k, where, :] for k in range(count)]
                )

    each_block(levels, per_group, block_of)


def pack_outer_kernel(
    here_ref, side_ref, pair_ref, step_ref, own_ref, outer_ref, sent_ref
):
    levels, _, width = pair_ref.shape
    bands = sent_ref.shape[0]
    halves = own_ref.shape[1] // SUB
    per_group = width // EDGE
    lanes = lax.broadcasted_iota(jnp.int32, (SUB, width), 1)
    mid = EDGE // 2
    lower = lanes % EDGE < mid
    eastern = (side_ref[0] + 1) % bands

    def block_of(block, counts):
        packed = []
        for i, count in enumerate(counts):
            group = block * GROUPS + i
            outer = pack_levels(
                lanes,
                [outer_rows(here_ref, pair_ref, step_ref, group * per_group + k)
                 for k in range(count)],
            )
            outer_ref[group] = outer
            packed.append(
                [own_ref[group, pl.ds(h * SUB, SUB), :] for h in range(halves)] + [outer]
            )
        for i in range(0, len(counts), 2):
            for part, (x, y) in enumerate(zip(packed[i], packed[i + 1])):
                last = jnp.where(lower, x, pltpu.roll(y, mid, 1))
                first = jnp.where(lower, pltpu.roll(x, width - mid, 1), y)
                both = block * (GROUPS // 2) + i // 2
                where = pl.ds(part * SUB, SUB)
                for band in range(bands):
                    sent_ref[band, both, where, :] = jnp.where(
                        eastern == band, last, first
                    ).astype(BF16)

    each_block(levels, per_group, block_of)


def around(parts, first, final):
    down = [pltpu.roll(x, 1, 0) for x in parts]
    up = [pltpu.roll(x, SUB - 1, 0) for x in parts]
    count = len(parts)
    return [
        jnp.where(first, down[i - 1], down[i]) + jnp.where(final, up[(i + 1) % count], up[i])
        for i in range(count)
    ]


def inside(here_ref, tiles, width):
    sub = lax.broadcasted_iota(jnp.int32, (SUB, width), 0)
    tile = here_ref[0]
    keep = jnp.where(
        sub < HALO, (tile < tiles - 1).astype(jnp.int32), (tile > 0).astype(jnp.int32)
    )
    return sub == 0, sub == SUB - 1, keep.astype(F32)


def main_kernel(tiles, here_ref, field_ref, pair_ref, step_ref, out_ref):
    levels, rows, width = field_ref.shape
    first, final, keep = inside(here_ref, tiles, width)

    def some_levels(block, carry):
        found = [block * BATCH + i for i in range(BATCH)]
        sets = [
            [field_ref[level, pl.ds(h * SUB, SUB), :] for h in range(rows // SUB)]
            + [outer_rows(here_ref, pair_ref, step_ref, level)]
            for level in found
        ]
        for _ in range(DIFF_STEPS):
            new = []
            for parts in sets:
                vertical = around(parts, first, final)
                parts = [
                    x + v + (pltpu.roll(x, 1, 1) + pltpu.roll(x, width - 1, 1))
                    for x, v in zip(parts, vertical)
                ]
                parts[-1] = parts[-1] * keep
                new.append(parts)
            sets = new
        for level, parts in zip(found, sets):
            for half, value in enumerate(parts[:-1]):
                out_ref[level, pl.ds(half * SUB, SUB), :] = value * step_scale
        return carry

    lax.fori_loop(0, levels // BATCH, some_levels, 0)


def edge_kernel(
    tiles, here_ref, side_ref, own_ref, outer_ref, got_ref, main_ref, out_ref
):
    levels, rows, width = main_ref.shape
    per_group = width // EDGE
    halves = rows // SUB
    first, final, keep = inside(here_ref, tiles, width)
    bands = got_ref.shape[0]
    western = (side_ref[0] + bands - 1) % bands
    eastern = (side_ref[0] + 1) % bands
    lanes = lax.broadcasted_iota(jnp.int32, (SUB, width), 1)
    column = lanes % EDGE
    mid = EDGE // 2
    last_own = column == mid - 1
    first_own = column == mid
    lower = column < mid
    touched = (lanes < HALO) | (lanes >= width - HALO)

    def block_of(block, counts):
        groups = [block * GROUPS + i for i in range(len(counts))]
        sets = [
            ([own_ref[group, pl.ds(h * SUB, SUB), :] for h in range(halves)]
             + [outer_ref[group]], [])
            for group in groups
        ]
        for i in range(0, len(groups), 2):
            both = block * (GROUPS // 2) + i // 2
            for part in range(halves + 1):
                where = pl.ds(part * SUB, SUB)
                west = got_ref[western, both, where, :].astype(F32)
                east = got_ref[eastern, both, where, :].astype(F32)
                sets[i][1].append(jnp.where(lower, west, pltpu.roll(east, mid, 1)))
                sets[i + 1][1].append(jnp.where(lower, pltpu.roll(west, width - mid, 1), east))
        for _ in range(DIFF_STEPS):
            new = []
            for own, other in sets:
                own_rows = around(own, first, final)
                other_rows = around(other, first, final)
                own_new, other_new = [], []
                for x, y, v, u in zip(own, other, own_rows, other_rows):
                    xe, ye = pltpu.roll(x, width - 1, 1), pltpu.roll(y, width - 1, 1)
                    xw, yw = pltpu.roll(x, 1, 1), pltpu.roll(y, 1, 1)
                    own_new.append(
                        x + v + (jnp.where(first_own, yw, xw) + jnp.where(last_own, ye, xe))
                    )
                    other_new.append(
                        y + u + (jnp.where(first_own, xw, yw) + jnp.where(last_own, xe, ye))
                    )
                own_new[-1] = own_new[-1] * keep
                other_new[-1] = other_new[-1] * keep
                new.append((own_new, other_new))
            sets = new
        for group, count, (own, _) in zip(groups, counts, sets):
            for half in range(halves):
                scaled = own[half] * step_scale
                where = pl.ds(half * SUB, SUB)
                for slot in range(count):
                    moved = pltpu.roll(scaled, (width - EDGE * slot - mid) % width, 1)
                    level = group * per_group + slot
                    out_ref[level, where, :] = jnp.where(
                        touched, moved, main_ref[level, where, :]
                    )

    each_block(levels, per_group, block_of)


def fast(shape, dtype):
    return pltpu.VMEM(shape, dtype)


def held(x):
    return pltpu.with_memory_space_constraint(x, pltpu.VMEM)


def swaps(size, first):
    return [pair for i in range(first, size - 1, 2) for pair in ((i, i + 1), (i + 1, i))]


def per_device(optical_depth, albedo, insolation, sunlit, point_weight, anomaly):
    rows, levels, points, width = optical_depth.shape
    tiles, bands = lax.axis_size("tiles"), lax.axis_size("band")
    here = lax.axis_index("tiles").astype(jnp.int32).reshape(1)
    side = lax.axis_index("band").astype(jnp.int32).reshape(1)
    planes = (levels, rows, width)
    edges = (levels, HALO, width)
    groups = -(-levels * EDGE // width)
    groups += groups % 2
    sweep = pltpu.VMEM((levels * rows * points, width), F32)
    heat, field, pair_edge, step_edge = pl.pallas_call(
        radiate_kernel,
        in_specs=[smem(), smem(), smem(), whole(), whole(), vmem(), whole()],
        out_specs=[whole()] + [vmem()] * 3,
        out_shape=[
            jax.ShapeDtypeStruct(planes, F32), fast(planes, F32), fast(edges, BF16),
            fast(edges, BF16),
        ],
        scratch_shapes=[sweep] * 3
        + [
            pltpu.VMEM(planes, F32),
            pltpu.VMEM(optical_depth.shape, BF16),
            pltpu.VMEM(planes, BF16),
            pltpu.VMEM(planes, F32),
            pltpu.VMEM(planes, F32),
            pltpu.SemaphoreType.DMA((levels // CHUNK,)),
            pltpu.SemaphoreType.DMA((2,)),
            pltpu.SemaphoreType.DMA((levels // CHUNK,)),
        ],
        name="radiate",
    )(
        here, point_weight, sunlit.reshape(rows), optical_depth, jnp.swapaxes(albedo, 0, 1),
        insolation, jnp.swapaxes(anomaly, 0, 1),
    )
    from_step = lax.ppermute(step_edge, "tiles", swaps(tiles, 1))
    from_pair = lax.ppermute(pair_edge, "tiles", swaps(tiles, 0))
    own = pl.pallas_call(
        pack_own_kernel,
        in_specs=[vmem()],
        out_specs=vmem(),
        out_shape=fast((groups, rows, width), F32),
        name="pack_own",
    )(held(field))
    outer, sent = pl.pallas_call(
        pack_outer_kernel,
        in_specs=[smem(), smem()] + [vmem()] * 3,
        out_specs=[vmem()] * 2,
        out_shape=[
            fast((groups, SUB, width), F32),
            fast((bands, groups // 2, rows + SUB, width), BF16),
        ],
        name="pack_outer",
    )(here, side, held(from_pair), held(from_step), held(own))
    got = lax.all_to_all(sent, "band", split_axis=0, concat_axis=0, tiled=True)
    inner = pl.pallas_call(
        functools.partial(main_kernel, tiles),
        in_specs=[smem()] + [vmem()] * 3,
        out_specs=vmem(),
        out_shape=fast(planes, F32),
        name="inner",
    )(here, held(field), held(from_pair), held(from_step))
    smoothed = pl.pallas_call(
        functools.partial(edge_kernel, tiles),
        in_specs=[smem(), smem()] + [vmem()] * 4,
        out_specs=vmem(),
        out_shape=jax.ShapeDtypeStruct(planes, F32),
        name="edge",
    )(here, side, held(own), held(outer), held(got), held(inner))
    return jnp.swapaxes(heat, 0, 1), jnp.swapaxes(smoothed, 0, 1)


def solution(mesh):
    placed = (
        P("tiles", None, None, "band"),
        P("tiles", None, "band"),
        P("tiles", "band"),
        P("tiles", "band"),
        P(),
        P("tiles", None, "band"),
    )
    return jax.shard_map(
        per_device,
        mesh=mesh,
        in_specs=placed,
        out_specs=(P("tiles", None, "band"), P("tiles", None, "band")),
        check_vma=False,
    )
```

```python
import functools
import math

import jax
import jax.numpy as jnp
from jax import lax
from jax.experimental import pallas as pl
from jax.experimental.pallas import tpu as pltpu
from jax.sharding import PartitionSpec as P

DIFF_STEPS = 4
BATCH = 18
GROUPS = 12
UNROLL_DOWN = 5
UNROLL_UP = 6
LIGHT_RATE = -2.0 * math.log2(math.e)
HALO = 4
EDGE = 16
SUB = 8
F32 = jnp.float32
BF16 = jnp.bfloat16
base_loss = 0.005
step_scale = 0.2**DIFF_STEPS


def vmem():
    return pl.BlockSpec(memory_space=pltpu.VMEM)


def smem():
    return pl.BlockSpec(memory_space=pltpu.SMEM)


def radiate_kernel(
    here_ref, weight_ref, lit_ref, depth_ref, albedo_ref, sun_ref, anomaly_ref,
    heat_ref, field_ref, pair_ref, step_ref,
    spread_ref, ratio_ref, swept_ref, extinct_ref,
):
    rows, levels, points, width = depth_ref.shape
    per_level = rows * points
    halves = rows // SUB
    chains = halves * points
    sun = sun_ref[...].astype(F32)
    row_ids = lax.broadcasted_iota(jnp.int32, (rows, width), 0)
    lit = jnp.zeros((rows, width), jnp.int32)
    for row in range(rows):
        lit = jnp.where(row_ids == row, lit_ref[row], lit)
    sun = jnp.where(lit == 1, sun, 0.0)
    suns = [sun[h * SUB:(h + 1) * SUB] for h in range(halves)]
    weights = [weight_ref[point] for point in range(points)]

    def spread(level):
        for row in range(rows):
            spread_ref[pl.ds(level * per_level + points * row, points), :] = (
                depth_ref[row, level].astype(F32)
            )

    def depth_of(level, half, point):
        start = level * per_level + half * SUB * points + point
        return spread_ref[pl.ds(start, SUB, stride=points), :]

    def albedo_of(level):
        both = albedo_ref[level].astype(F32)
        return [both[h * SUB:(h + 1) * SUB] for h in range(halves)]

    def place(level, chain):
        return pl.ds(pl.multiple_of(level * per_level + chain * SUB, SUB), SUB)

    zero = jnp.zeros((SUB, width), F32)
    one = jnp.ones((SUB, width), F32)

    def down(level, carry):
        link_prev, albedo_now, depth, light, ratio, swept = carry
        last = level == levels - 1
        following = jnp.where(last, level, level + 1)
        spread(following)
        albedo_next = albedo_of(following)
        out = ([], [], [], [], [])
        for half in range(halves):
            albedo = albedo_now[half]
            before = link_prev[half]
            link = jnp.where(last, 0.0, albedo * albedo_next[half])
            slope = 2.0 * (1.0 - albedo)
            level_part = base_loss + before + link
            direct = None
            for point in range(points):
                chain = half * points + point
                layer = depth_of(level, half, point)
                depth_new = depth[chain] + layer
                light_new = jnp.exp2(depth_new * LIGHT_RATE)
                extinct = weights[point] * (light[chain] - light_new)
                direct = extinct if direct is None else direct + extinct
                inverse = 1.0 / (level_part + slope * layer - before * ratio[chain])
                ratio_new = link * inverse
                swept_new = (albedo * extinct + before * swept[chain]) * inverse
                where = place(level, chain)
                ratio_ref[where, :] = ratio_new
                swept_ref[where, :] = swept_new
                for item, value in zip(out, (depth_new, light_new, ratio_new, swept_new)):
                    item.append(value)
            out[4].append(link)
            extinct_ref[level, pl.ds(half * SUB, SUB), :] = direct
        return (
            tuple(out[4]), tuple(albedo_next), tuple(out[0]), tuple(out[1]), tuple(out[2]),
            tuple(out[3]),
        )

    spread(0)
    lax.fori_loop(
        0, levels, down,
        ((zero,) * halves, tuple(albedo_of(0)), (zero,) * chains, (one,) * chains,
         (zero,) * chains, (zero,) * chains),
        unroll=UNROLL_DOWN,
    )
    even = here_ref[0] % 2 == 0

    def up(i, flux):
        level = levels - 1 - i
        albedos = albedo_of(level)
        flux_new = []
        fields = []
        for half in range(halves):
            total = None
            for point in range(points):
                chain = half * points + point
                where = place(level, chain)
                diffuse = swept_ref[where, :] + ratio_ref[where, :] * flux[chain]
                flux_new.append(diffuse)
                term = depth_of(level, half, point) * diffuse
                total = term if total is None else total + term
            part = pl.ds(half * SUB, SUB)
            absorbed = extinct_ref[level, part, :] + 2.0 * total
            heat = suns[half] * ((1.0 - albedos[half]) * absorbed)
            heat_ref[level, part, :] = heat
            field = anomaly_ref[level, part, :] + heat
            field_ref[level, part, :] = field
            fields.append(field)
        top, bottom = fields[0][:HALO], fields[-1][SUB - HALO:]
        pair_ref[level] = jnp.where(even, bottom, top).astype(BF16)
        step_ref[level] = jnp.where(even, top, bottom).astype(BF16)
        return tuple(flux_new)

    lax.fori_loop(0, levels, up, (zero,) * chains, unroll=UNROLL_UP)


def outer_rows(here_ref, pair_ref, step_ref, level):
    pair, step = pair_ref[level].astype(F32), step_ref[level].astype(F32)
    even = here_ref[0] % 2 == 0
    below = jnp.where(even, pair, step)
    above = jnp.where(even, step, pair)
    return jnp.concatenate([below, above], axis=0)


def pack_levels(lanes, parts):
    width = lanes.shape[1]
    packed = None
    for slot, part in enumerate(parts):
        moved = pltpu.roll(part, (EDGE * slot + EDGE // 2) % width, 1)
        packed = moved if packed is None else jnp.where(lanes >= EDGE * slot, moved, packed)
    return packed


def each_block(levels, per_group, body):
    full = levels // per_group
    counts = [per_group] * full + ([levels % per_group] if levels % per_group else [])
    blocks = full // GROUPS
    lax.fori_loop(0, blocks, lambda b, c: (body(b, counts[:GROUPS]), c)[1], 0)
    if counts[blocks * GROUPS:]:
        body(blocks, counts[blocks * GROUPS:])


def pack_own_kernel(field_ref, packed_ref):
    levels, rows, width = field_ref.shape
    per_group = width // EDGE
    lanes = lax.broadcasted_iota(jnp.int32, (SUB, width), 1)

    def block_of(block, counts):
        for i, count in enumerate(counts):
            group = block * GROUPS + i
            for half in range(rows // SUB):
                where = pl.ds(half * SUB, SUB)
                packed_ref[group, where, :] = pack_levels(
                    lanes, [field_ref[group * per_group + k, where, :] for k in range(count)]
                )

    each_block(levels, per_group, block_of)


def pack_outer_kernel(
    here_ref, side_ref, pair_ref, step_ref, own_ref, outer_ref, near_ref, far_ref
):
    levels, _, width = pair_ref.shape
    halves = own_ref.shape[1] // SUB
    per_group = width // EDGE
    lanes = lax.broadcasted_iota(jnp.int32, (SUB, width), 1)
    mid = EDGE // 2
    lower = lanes % EDGE < mid
    even = side_ref[0] % 2 == 0

    def block_of(block, counts):
        packed = []
        for i, count in enumerate(counts):
            group = block * GROUPS + i
            outer = pack_levels(
                lanes,
                [outer_rows(here_ref, pair_ref, step_ref, group * per_group + k)
                 for k in range(count)],
            )
            outer_ref[group] = outer
            packed.append(
                [own_ref[group, pl.ds(h * SUB, SUB), :] for h in range(halves)] + [outer]
            )
        for i in range(0, len(counts), 2):
            for part, (x, y) in enumerate(zip(packed[i], packed[i + 1])):
                last = jnp.where(lower, x, pltpu.roll(y, mid, 1))
                first = jnp.where(lower, pltpu.roll(x, width - mid, 1), y)
                both = block * (GROUPS // 2) + i // 2
                where = pl.ds(part * SUB, SUB)
                near_ref[both, where, :] = jnp.where(even, last, first).astype(BF16)
                far_ref[both, where, :] = jnp.where(even, first, last).astype(BF16)

    each_block(levels, per_group, block_of)


def around(parts, first, final):
    down = [pltpu.roll(x, 1, 0) for x in parts]
    up = [pltpu.roll(x, SUB - 1, 0) for x in parts]
    count = len(parts)
    return [
        jnp.where(first, down[i - 1], down[i]) + jnp.where(final, up[(i + 1) % count], up[i])
        for i in range(count)
    ]


def inside(here_ref, tiles, width):
    sub = lax.broadcasted_iota(jnp.int32, (SUB, width), 0)
    tile = here_ref[0]
    keep = jnp.where(
        sub < HALO, (tile < tiles - 1).astype(jnp.int32), (tile > 0).astype(jnp.int32)
    )
    return sub == 0, sub == SUB - 1, keep.astype(F32)


def main_kernel(tiles, here_ref, field_ref, pair_ref, step_ref, out_ref):
    levels, rows, width = field_ref.shape
    first, final, keep = inside(here_ref, tiles, width)

    def some_levels(block, carry):
        found = [block * BATCH + i for i in range(BATCH)]
        sets = [
            [field_ref[level, pl.ds(h * SUB, SUB), :] for h in range(rows // SUB)]
            + [outer_rows(here_ref, pair_ref, step_ref, level)]
            for level in found
        ]
        for _ in range(DIFF_STEPS):
            new = []
            for parts in sets:
                vertical = around(parts, first, final)
                parts = [
                    x + v + (pltpu.roll(x, 1, 1) + pltpu.roll(x, width - 1, 1))
                    for x, v in zip(parts, vertical)
                ]
                parts[-1] = parts[-1] * keep
                new.append(parts)
            sets = new
        for level, parts in zip(found, sets):
            for half, value in enumerate(parts[:-1]):
                out_ref[level, pl.ds(half * SUB, SUB), :] = value * step_scale
        return carry

    lax.fori_loop(0, levels // BATCH, some_levels, 0)


def edge_kernel(
    tiles, here_ref, side_ref, own_ref, outer_ref, near_ref, far_ref, main_ref, out_ref
):
    levels, rows, width = main_ref.shape
    per_group = width // EDGE
    halves = rows // SUB
    first, final, keep = inside(here_ref, tiles, width)
    even = side_ref[0] % 2 == 0
    lanes = lax.broadcasted_iota(jnp.int32, (SUB, width), 1)
    column = lanes % EDGE
    mid = EDGE // 2
    last_own = column == mid - 1
    first_own = column == mid
    lower = column < mid
    touched = (lanes < HALO) | (lanes >= width - HALO)

    def block_of(block, counts):
        groups = [block * GROUPS + i for i in range(len(counts))]
        sets = [
            ([own_ref[group, pl.ds(h * SUB, SUB), :] for h in range(halves)]
             + [outer_ref[group]], [])
            for group in groups
        ]
        for i in range(0, len(groups), 2):
            both = block * (GROUPS // 2) + i // 2
            for part in range(halves + 1):
                where = pl.ds(part * SUB, SUB)
                near = near_ref[both, where, :].astype(F32)
                far = far_ref[both, where, :].astype(F32)
                west, east = jnp.where(even, far, near), jnp.where(even, near, far)
                sets[i][1].append(jnp.where(lower, west, pltpu.roll(east, mid, 1)))
                sets[i + 1][1].append(jnp.where(lower, pltpu.roll(west, width - mid, 1), east))
        for _ in range(DIFF_STEPS):
            new = []
            for own, other in sets:
                own_rows = around(own, first, final)
                other_rows = around(other, first, final)
                own_new, other_new = [], []
                for x, y, v, u in zip(own, other, own_rows, other_rows):
                    xe, ye = pltpu.roll(x, width - 1, 1), pltpu.roll(y, width - 1, 1)
                    xw, yw = pltpu.roll(x, 1, 1), pltpu.roll(y, 1, 1)
                    own_new.append(
                        x + v + (jnp.where(first_own, yw, xw) + jnp.where(last_own, ye, xe))
                    )
                    other_new.append(
                        y + u + (jnp.where(first_own, xw, yw) + jnp.where(last_own, xe, ye))
                    )
                own_new[-1] = own_new[-1] * keep
                other_new[-1] = other_new[-1] * keep
                new.append((own_new, other_new))
            sets = new
        for group, count, (own, _) in zip(groups, counts, sets):
            for half in range(halves):
                scaled = own[half] * step_scale
                where = pl.ds(half * SUB, SUB)
                for slot in range(count):
                    moved = pltpu.roll(scaled, (width - EDGE * slot - mid) % width, 1)
                    level = group * per_group + slot
                    out_ref[level, where, :] = jnp.where(
                        touched, moved, main_ref[level, where, :]
                    )

    each_block(levels, per_group, block_of)


def fast(shape, dtype):
    return pltpu.VMEM(shape, dtype)


def held(x):
    return pltpu.with_memory_space_constraint(x, pltpu.VMEM)


def swaps(size, first, ring):
    ends = range(first, size if ring else size - 1, 2)
    return [pair for i in ends for pair in ((i, (i + 1) % size), ((i + 1) % size, i))]


def per_device(optical_depth, albedo, insolation, sunlit, point_weight, anomaly):
    rows, levels, points, width = optical_depth.shape
    tiles, bands = lax.axis_size("tiles"), lax.axis_size("band")
    here = lax.axis_index("tiles").astype(jnp.int32).reshape(1)
    side = lax.axis_index("band").astype(jnp.int32).reshape(1)
    planes = (levels, rows, width)
    edges = (levels, HALO, width)
    groups = -(-levels * EDGE // width)
    groups += groups % 2
    sweep = pltpu.VMEM((levels * rows * points, width), F32)
    heat, field, pair_edge, step_edge = pl.pallas_call(
        radiate_kernel,
        in_specs=[smem(), smem(), smem(), vmem(), vmem(), vmem(), vmem()],
        out_specs=[vmem()] * 4,
        out_shape=[
            jax.ShapeDtypeStruct(planes, F32), fast(planes, F32), fast(edges, BF16),
            fast(edges, BF16),
        ],
        scratch_shapes=[sweep] * 3 + [pltpu.VMEM(planes, F32)],
        name="radiate",
    )(
        here, point_weight, sunlit.reshape(rows), optical_depth, jnp.swapaxes(albedo, 0, 1),
        insolation, jnp.swapaxes(anomaly, 0, 1),
    )
    from_step = lax.ppermute(step_edge, "tiles", swaps(tiles, 1, False))
    from_pair = lax.ppermute(pair_edge, "tiles", swaps(tiles, 0, False))
    own = pl.pallas_call(
        pack_own_kernel,
        in_specs=[vmem()],
        out_specs=vmem(),
        out_shape=fast((groups, rows, width), F32),
        name="pack_own",
    )(held(field))
    sent = fast((groups // 2, rows + SUB, width), BF16)
    outer, to_near, to_far = pl.pallas_call(
        pack_outer_kernel,
        in_specs=[smem(), smem()] + [vmem()] * 3,
        out_specs=[vmem()] * 3,
        out_shape=[fast((groups, SUB, width), F32), sent, sent],
        name="pack_outer",
    )(here, side, held(from_pair), held(from_step), held(own))
    far = lax.ppermute(to_far, "band", swaps(bands, 1, True))
    near = lax.ppermute(to_near, "band", swaps(bands, 0, True))
    inner = pl.pallas_call(
        functools.partial(main_kernel, tiles),
        in_specs=[smem()] + [vmem()] * 3,
        out_specs=vmem(),
        out_shape=fast(planes, F32),
        name="inner",
    )(here, held(field), held(from_pair), held(from_step))
    smoothed = pl.pallas_call(
        functools.partial(edge_kernel, tiles),
        in_specs=[smem(), smem()] + [vmem()] * 5,
        out_specs=vmem(),
        out_shape=jax.ShapeDtypeStruct(planes, F32),
        name="edge",
    )(here, side, held(own), held(outer), held(near), held(far), held(inner))
    return jnp.swapaxes(heat, 0, 1), jnp.swapaxes(smoothed, 0, 1)


def solution(mesh):
    placed = (
        P("tiles", None, None, "band"),
        P("tiles", None, "band"),
        P("tiles", "band"),
        P("tiles", "band"),
        P(),
        P("tiles", None, "band"),
    )
    return jax.shard_map(
        per_device,
        mesh=mesh,
        in_specs=placed,
        out_specs=(P("tiles", None, "band"), P("tiles", None, "band")),
        check_vma=False,
    )
```

```python
import functools
import math

import jax
import jax.numpy as jnp
from jax import lax
from jax.experimental import pallas as pl
from jax.experimental.pallas import tpu as pltpu
from jax.sharding import PartitionSpec as P

DIFF_STEPS = 4
RING = 24
BATCH = 18
GROUPS = 12
UNROLL_DOWN = 5
UNROLL_UP = 6
LIGHT_RATE = -2.0 * math.log2(math.e)
HALO = 4
EDGE = 16
SUB = 8
F32 = jnp.float32
BF16 = jnp.bfloat16
base_loss = 0.005
step_scale = 0.2**DIFF_STEPS


def vmem():
    return pl.BlockSpec(memory_space=pltpu.VMEM)


def smem():
    return pl.BlockSpec(memory_space=pltpu.SMEM)


def radiate_kernel(
    here_ref, weight_ref, lit_ref, depth_ref, albedo_ref, sun_ref, anomaly_ref,
    heat_ref, field_ref, pair_ref, step_ref,
    spread_ref, ratio_ref, swept_ref, extinct_ref,
):
    rows, levels, points, width = depth_ref.shape
    per_level = rows * points
    halves = rows // SUB
    chains = halves * points
    sun = sun_ref[...].astype(F32)
    row_ids = lax.broadcasted_iota(jnp.int32, (rows, width), 0)
    lit = jnp.zeros((rows, width), jnp.int32)
    for row in range(rows):
        lit = jnp.where(row_ids == row, lit_ref[row], lit)
    sun = jnp.where(lit == 1, sun, 0.0)
    suns = [sun[h * SUB:(h + 1) * SUB] for h in range(halves)]
    weights = [weight_ref[point] for point in range(points)]

    def spread(level):
        for row in range(rows):
            spread_ref[pl.ds(level * per_level + points * row, points), :] = (
                depth_ref[row, level].astype(F32)
            )

    def depth_of(level, half, point):
        start = level * per_level + half * SUB * points + point
        return spread_ref[pl.ds(start, SUB, stride=points), :]

    def albedo_of(level):
        both = albedo_ref[level].astype(F32)
        return [both[h * SUB:(h + 1) * SUB] for h in range(halves)]

    def place(level, chain):
        return pl.ds(pl.multiple_of(level * per_level + chain * SUB, SUB), SUB)

    zero = jnp.zeros((SUB, width), F32)
    one = jnp.ones((SUB, width), F32)

    def down(level, carry):
        link_prev, albedo_now, depth, light, ratio, swept = carry
        last = level == levels - 1
        following = jnp.where(last, level, level + 1)
        spread(following)
        albedo_next = albedo_of(following)
        out = ([], [], [], [], [])
        for half in range(halves):
            albedo = albedo_now[half]
            before = link_prev[half]
            link = jnp.where(last, 0.0, albedo * albedo_next[half])
            slope = 2.0 * (1.0 - albedo)
            level_part = base_loss + before + link
            direct = None
            for point in range(points):
                chain = half * points + point
                layer = depth_of(level, half, point)
                depth_new = depth[chain] + layer
                light_new = jnp.exp2(depth_new * LIGHT_RATE)
                extinct = weights[point] * (light[chain] - light_new)
                direct = extinct if direct is None else direct + extinct
                inverse = 1.0 / (level_part + slope * layer - before * ratio[chain])
                ratio_new = link * inverse
                swept_new = (albedo * extinct + before * swept[chain]) * inverse
                where = place(level, chain)
                ratio_ref[where, :] = ratio_new
                swept_ref[where, :] = swept_new
                for item, value in zip(out, (depth_new, light_new, ratio_new, swept_new)):
                    item.append(value)
            out[4].append(link)
            extinct_ref[level, pl.ds(half * SUB, SUB), :] = direct
        return (
            tuple(out[4]), tuple(albedo_next), tuple(out[0]), tuple(out[1]), tuple(out[2]),
            tuple(out[3]),
        )

    spread(0)
    lax.fori_loop(
        0, levels, down,
        ((zero,) * halves, tuple(albedo_of(0)), (zero,) * chains, (one,) * chains,
         (zero,) * chains, (zero,) * chains),
        unroll=UNROLL_DOWN,
    )
    even = here_ref[0] % 2 == 0

    def up(i, flux):
        level = levels - 1 - i
        albedos = albedo_of(level)
        flux_new = []
        fields = []
        for half in range(halves):
            total = None
            for point in range(points):
                chain = half * points + point
                where = place(level, chain)
                diffuse = swept_ref[where, :] + ratio_ref[where, :] * flux[chain]
                flux_new.append(diffuse)
                term = depth_of(level, half, point) * diffuse
                total = term if total is None else total + term
            part = pl.ds(half * SUB, SUB)
            absorbed = extinct_ref[level, part, :] + 2.0 * total
            heat = suns[half] * ((1.0 - albedos[half]) * absorbed)
            heat_ref[level, part, :] = heat
            field = anomaly_ref[level, part, :] + heat
            field_ref[level, part, :] = field
            fields.append(field)
        top, bottom = fields[0][:HALO], fields[-1][SUB - HALO:]
        pair_ref[level] = jnp.where(even, bottom, top).astype(BF16)
        step_ref[level] = jnp.where(even, top, bottom).astype(BF16)
        return tuple(flux_new)

    lax.fori_loop(0, levels, up, (zero,) * chains, unroll=UNROLL_UP)


def outer_rows(here_ref, pair_ref, late_ref, step_ref, level):
    pair = pair_ref[level].astype(F32) + late_ref[level].astype(F32)
    step = step_ref[level].astype(F32)
    even = here_ref[0] % 2 == 0
    below = jnp.where(even, pair, step)
    above = jnp.where(even, step, pair)
    return jnp.concatenate([below, above], axis=0)


def pack_levels(lanes, parts):
    width = lanes.shape[1]
    packed = None
    for slot, part in enumerate(parts):
        moved = pltpu.roll(part, (EDGE * slot + EDGE // 2) % width, 1)
        packed = moved if packed is None else jnp.where(lanes >= EDGE * slot, moved, packed)
    return packed


def each_block(levels, per_group, body):
    full = levels // per_group
    counts = [per_group] * full + ([levels % per_group] if levels % per_group else [])
    blocks = full // GROUPS
    lax.fori_loop(0, blocks, lambda b, c: (body(b, counts[:GROUPS]), c)[1], 0)
    if counts[blocks * GROUPS:]:
        body(blocks, counts[blocks * GROUPS:])


def pack_own_kernel(field_ref, packed_ref):
    levels, rows, width = field_ref.shape
    per_group = width // EDGE
    lanes = lax.broadcasted_iota(jnp.int32, (SUB, width), 1)

    def block_of(block, counts):
        for i, count in enumerate(counts):
            group = block * GROUPS + i
            for half in range(rows // SUB):
                where = pl.ds(half * SUB, SUB)
                packed_ref[group, where, :] = pack_levels(
                    lanes, [field_ref[group * per_group + k, where, :] for k in range(count)]
                )

    each_block(levels, per_group, block_of)


def pack_outer_kernel(
    here_ref, side_ref, pair_ref, late_ref, step_ref, own_ref, outer_ref, near_ref, far_ref
):
    levels, _, width = pair_ref.shape
    halves = own_ref.shape[1] // SUB
    per_group = width // EDGE
    lanes = lax.broadcasted_iota(jnp.int32, (SUB, width), 1)
    mid = EDGE // 2
    lower = lanes % EDGE < mid
    even = side_ref[0] % 2 == 0

    def block_of(block, counts):
        packed = []
        for i, count in enumerate(counts):
            group = block * GROUPS + i
            outer = pack_levels(
                lanes,
                [outer_rows(here_ref, pair_ref, late_ref, step_ref, group * per_group + k)
                 for k in range(count)],
            )
            outer_ref[group] = outer
            packed.append(
                [own_ref[group, pl.ds(h * SUB, SUB), :] for h in range(halves)] + [outer]
            )
        for i in range(0, len(counts), 2):
            for part, (x, y) in enumerate(zip(packed[i], packed[i + 1])):
                last = jnp.where(lower, x, pltpu.roll(y, mid, 1))
                first = jnp.where(lower, pltpu.roll(x, width - mid, 1), y)
                both = block * (GROUPS // 2) + i // 2
                where = pl.ds(part * SUB, SUB)
                near_ref[both, where, :] = jnp.where(even, last, first).astype(BF16)
                far_ref[both, where, :] = jnp.where(even, first, last).astype(BF16)

    each_block(levels, per_group, block_of)


def around(parts, first, final):
    down = [pltpu.roll(x, 1, 0) for x in parts]
    up = [pltpu.roll(x, SUB - 1, 0) for x in parts]
    count = len(parts)
    return [
        jnp.where(first, down[i - 1], down[i]) + jnp.where(final, up[(i + 1) % count], up[i])
        for i in range(count)
    ]


def inside(here_ref, tiles, width):
    sub = lax.broadcasted_iota(jnp.int32, (SUB, width), 0)
    tile = here_ref[0]
    keep = jnp.where(
        sub < HALO, (tile < tiles - 1).astype(jnp.int32), (tile > 0).astype(jnp.int32)
    )
    return sub == 0, sub == SUB - 1, keep.astype(F32)


def main_kernel(tiles, here_ref, field_ref, pair_ref, late_ref, step_ref, out_ref):
    levels, rows, width = field_ref.shape
    first, final, keep = inside(here_ref, tiles, width)

    def some_levels(block, carry):
        found = [block * BATCH + i for i in range(BATCH)]
        sets = [
            [field_ref[level, pl.ds(h * SUB, SUB), :] for h in range(rows // SUB)]
            + [outer_rows(here_ref, pair_ref, late_ref, step_ref, level)]
            for level in found
        ]
        for _ in range(DIFF_STEPS):
            new = []
            for parts in sets:
                vertical = around(parts, first, final)
                parts = [
                    x + v + (pltpu.roll(x, 1, 1) + pltpu.roll(x, width - 1, 1))
                    for x, v in zip(parts, vertical)
                ]
                parts[-1] = parts[-1] * keep
                new.append(parts)
            sets = new
        for level, parts in zip(found, sets):
            for half, value in enumerate(parts[:-1]):
                out_ref[level, pl.ds(half * SUB, SUB), :] = value * step_scale
        return carry

    lax.fori_loop(0, levels // BATCH, some_levels, 0)


def edge_kernel(
    tiles, here_ref, side_ref, own_ref, outer_ref, near_ref, far_ref, main_ref, out_ref
):
    levels, rows, width = main_ref.shape
    per_group = width // EDGE
    halves = rows // SUB
    first, final, keep = inside(here_ref, tiles, width)
    even = side_ref[0] % 2 == 0
    lanes = lax.broadcasted_iota(jnp.int32, (SUB, width), 1)
    column = lanes % EDGE
    mid = EDGE // 2
    last_own = column == mid - 1
    first_own = column == mid
    lower = column < mid
    touched = (lanes < HALO) | (lanes >= width - HALO)

    def block_of(block, counts):
        groups = [block * GROUPS + i for i in range(len(counts))]
        sets = [
            ([own_ref[group, pl.ds(h * SUB, SUB), :] for h in range(halves)]
             + [outer_ref[group]], [])
            for group in groups
        ]
        for i in range(0, len(groups), 2):
            both = block * (GROUPS // 2) + i // 2
            for part in range(halves + 1):
                where = pl.ds(part * SUB, SUB)
                near = near_ref[both, where, :].astype(F32)
                far = far_ref[both, where, :].astype(F32)
                west, east = jnp.where(even, far, near), jnp.where(even, near, far)
                sets[i][1].append(jnp.where(lower, west, pltpu.roll(east, mid, 1)))
                sets[i + 1][1].append(jnp.where(lower, pltpu.roll(west, width - mid, 1), east))
        for _ in range(DIFF_STEPS):
            new = []
            for own, other in sets:
                own_rows = around(own, first, final)
                other_rows = around(other, first, final)
                own_new, other_new = [], []
                for x, y, v, u in zip(own, other, own_rows, other_rows):
                    xe, ye = pltpu.roll(x, width - 1, 1), pltpu.roll(y, width - 1, 1)
                    xw, yw = pltpu.roll(x, 1, 1), pltpu.roll(y, 1, 1)
                    own_new.append(
                        x + v + (jnp.where(first_own, yw, xw) + jnp.where(last_own, ye, xe))
                    )
                    other_new.append(
                        y + u + (jnp.where(first_own, xw, yw) + jnp.where(last_own, xe, ye))
                    )
                own_new[-1] = own_new[-1] * keep
                other_new[-1] = other_new[-1] * keep
                new.append((own_new, other_new))
            sets = new
        for group, count, (own, _) in zip(groups, counts, sets):
            for half in range(halves):
                scaled = own[half] * step_scale
                where = pl.ds(half * SUB, SUB)
                for slot in range(count):
                    moved = pltpu.roll(scaled, (width - EDGE * slot - mid) % width, 1)
                    level = group * per_group + slot
                    out_ref[level, where, :] = jnp.where(
                        touched, moved, main_ref[level, where, :]
                    )

    each_block(levels, per_group, block_of)


def fast(shape, dtype):
    return pltpu.VMEM(shape, dtype)


def held(x):
    return pltpu.with_memory_space_constraint(x, pltpu.VMEM)


def swaps(size, first, ring):
    ends = range(first, size if ring else size - 1, 2)
    return [pair for i in ends for pair in ((i, (i + 1) % size), ((i + 1) % size, i))]


def per_device(optical_depth, albedo, insolation, sunlit, point_weight, anomaly):
    rows, levels, points, width = optical_depth.shape
    tiles, bands = lax.axis_size("tiles"), lax.axis_size("band")
    here = lax.axis_index("tiles").astype(jnp.int32).reshape(1)
    side = lax.axis_index("band").astype(jnp.int32).reshape(1)
    planes = (levels, rows, width)
    edges = (levels, HALO, width)
    groups = -(-levels * EDGE // width)
    groups += groups % 2
    sweep = pltpu.VMEM((levels * rows * points, width), F32)
    heat, field, pair_edge, step_edge = pl.pallas_call(
        radiate_kernel,
        in_specs=[smem(), smem(), smem(), vmem(), vmem(), vmem(), vmem()],
        out_specs=[vmem()] * 4,
        out_shape=[
            jax.ShapeDtypeStruct(planes, F32), fast(planes, F32), fast(edges, BF16),
            fast(edges, BF16),
        ],
        scratch_shapes=[sweep] * 3 + [pltpu.VMEM(planes, F32)],
        name="radiate",
    )(
        here, point_weight, sunlit.reshape(rows), optical_depth, jnp.swapaxes(albedo, 0, 1),
        insolation, jnp.swapaxes(anomaly, 0, 1),
    )
    from_step = lax.ppermute(step_edge, "tiles", swaps(tiles, 1, False))
    pairs = swaps(tiles, 0, False)
    from_pair = lax.ppermute(pair_edge, "tiles", [p for p in pairs if p[0] % RING < RING // 2])
    from_late = lax.ppermute(pair_edge, "tiles", [p for p in pairs if p[0] % RING >= RING // 2])
    own = pl.pallas_call(
        pack_own_kernel,
        in_specs=[vmem()],
        out_specs=vmem(),
        out_shape=fast((groups, rows, width), F32),
        name="pack_own",
    )(held(field))
    sent = fast((groups // 2, rows + SUB, width), BF16)
    outer, to_near, to_far = pl.pallas_call(
        pack_outer_kernel,
        in_specs=[smem(), smem()] + [vmem()] * 4,
        out_specs=[vmem()] * 3,
        out_shape=[fast((groups, SUB, width), F32), sent, sent],
        name="pack_outer",
    )(here, side, held(from_pair), held(from_late), held(from_step), held(own))
    near = lax.ppermute(to_near, "band", swaps(bands, 0, True))
    far = lax.ppermute(to_far, "band", swaps(bands, 1, True))
    inner = pl.pallas_call(
        functools.partial(main_kernel, tiles),
        in_specs=[smem()] + [vmem()] * 4,
        out_specs=vmem(),
        out_shape=fast(planes, F32),
        name="inner",
    )(here, held(field), held(from_pair), held(from_late), held(from_step))
    smoothed = pl.pallas_call(
        functools.partial(edge_kernel, tiles),
        in_specs=[smem(), smem()] + [vmem()] * 5,
        out_specs=vmem(),
        out_shape=jax.ShapeDtypeStruct(planes, F32),
        name="edge",
    )(here, side, held(own), held(outer), held(near), held(far), held(inner))
    return jnp.swapaxes(heat, 0, 1), jnp.swapaxes(smoothed, 0, 1)


def solution(mesh):
    placed = (
        P("tiles", None, None, "band"),
        P("tiles", None, "band"),
        P("tiles", "band"),
        P("tiles", "band"),
        P(),
        P("tiles", None, "band"),
    )
    return jax.shard_map(
        per_device,
        mesh=mesh,
        in_specs=placed,
        out_specs=(P("tiles", None, "band"), P("tiles", None, "band")),
        check_vma=False,
    )
```
